32 devices in a mesh: seq: 4 (over z), ctx: 8 (over y, x, core).
Axes of the slice: x: 2, y: 2, z: 4, core: 2. Of those that a mesh axis runs over, the one named last changes fastest.
Arguments:
- queries: bfloat16 [4, 4096, 2048], P('seq', 'ctx'), may hold values from -64 to 64
- keys: bfloat16 [4, 4096, 2048], P('seq', 'ctx'), may hold values from -6 to 6
- values: bfloat16 [4, 4096, 2048], P('seq', 'ctx'), may hold values from -6 to 6
- out_grad: bfloat16 [4, 4096, 2048], P('seq', 'ctx'), may hold values from -6 to 6
- cluster_ids: int32 [4, 16, 4096, 1], P('seq', None, 'ctx'), may hold values from 0 to 63; in each aligned block of 512 rows (0 to 511, 512 to 1023, ..., all dimensions but the last counted through in order) at most 16 rows name the same one
- centroids: float32 [16, 64, 128], replicated, may hold values from -6 to 6
Outputs:
- grad_queries: bfloat16 [4, 4096, 2048], P('seq', 'ctx')
- grad_keys: bfloat16 [4, 4096, 2048], P('seq', 'ctx')
- grad_values: bfloat16 [4, 4096, 2048], P('seq', 'ctx')
- new_centroids: float32 [16, 64, 128], P('ctx')
The draws below stay inside these ranges and needn't reach their ends.
Inputs may be any that keep to these rules, and one draw needn't show every extreme that they name: `cluster_ids`: in each sequence and head, no cluster holds more than 16 of the 512 tokens of one index of ctx; some cluster holds exactly 16 in some such block.
All inputs are finite; a program needn't handle non-finite values.
Results may differ from the reference program's by a relative error of at most 0.0052.
Values may be sent and summed in bfloat16 or wider, within the bound.
A program may use at most 192 MiB of HBM per device.

```python
import math
import jax
import jax.numpy as jnp
import numpy as np
from jax import lax

H = 16
DH = 128
CLUSTERS = 64
TOK_DEV = 512
CAP = 16
SEQS = 4
LEN = 4096
N_CTX = 8


def paired_draw(key):
    base = jax.random.fold_in(key, 11)
    first, second = jax.random.split(base, 2)
    shape = (SEQS, LEN, H, DH)
    key_vals = jnp.clip(jax.random.normal(second, shape, jnp.float32), -6.0, 6.0)
    query_vals = jnp.clip(jax.random.normal(first, shape, jnp.float32), -6.0, 6.0)
    return (query_vals.reshape(SEQS, LEN, H * DH), key_vals.reshape(SEQS, LEN, H * DH))


def draw_queries(key, part):
    return paired_draw(key)[0].astype(jnp.bfloat16)


def draw_keys(key, part):
    return paired_draw(key)[1].astype(jnp.bfloat16)


def shard_levels(own_key, dims, cuts, least, top_value):
    factor_of = 1.0
    for axis_at, shards_of in cuts:
        steps = jax.random.uniform(jax.random.fold_in(jax.random.fold_in(own_key, 6), axis_at), (shards_of,), jnp.float32, least / len(cuts), top_value / len(cuts))
        factor_of = factor_of * jnp.repeat(jnp.exp(steps), dims[axis_at] // shards_of).reshape((-1,) + (1,) * (len(dims) - 1 - axis_at))
    return factor_of


def routed_block(own_key, own, number, rows, amount, top, most, slope):
    ranking = jax.random.permutation(own_key, amount)
    crowded, usual = load_shares(amount, rows * top, most, slope, True), load_shares(amount, rows * top, most, slope, False)
    places = jnp.arange(amount)

    def named(lengths, rotation):
        used = int((lengths > 0).sum())
        fixed = max(1, used // 4)
        moved = fixed + (places - fixed + rotation * (used - fixed)) % max(1, amount - fixed)
        return jnp.zeros((amount,), jnp.int32).at[ranking[jnp.where(places < fixed, places, moved)]].set(jnp.asarray(lengths, jnp.int32))

    lengths = jnp.where(number % 4 == 0, named(crowded, number // 4), named(usual, number - number // 4 - 1))
    mixed = jax.random.permutation(jax.random.fold_in(own, 3), amount)
    donor, taker = mixed[0:amount // 2 * 2:2], mixed[1:amount // 2 * 2:2]
    slack = jnp.minimum(lengths[donor] - 1, most - lengths[taker]) // 2
    slack = jnp.where((donor == ranking[0]) | (taker == ranking[0]) | (lengths[taker] == 0), 0, jnp.maximum(slack, 0))
    moved = jax.random.randint(jax.random.fold_in(own, 4), (amount // 2,), 0, 1 << 20) % (slack + 1)
    lengths = lengths.at[donor].add(-moved).at[taker].add(moved)
    members = jnp.searchsorted(jnp.cumsum(lengths), jnp.arange(rows * top), side="right").astype(jnp.int32)
    table = members.reshape(top, rows).T
    table = table[jax.random.permutation(jax.random.fold_in(own, 1), rows)]
    rotation = jax.random.randint(jax.random.fold_in(own, 2), (rows, 1), 0, top)
    return jnp.take_along_axis(table, (jnp.arange(top)[None, :] + rotation) % top, axis=1)


def load_shares(number_of, total, reach, slope, full):
    weights = [(1 << 20) // math.isqrt(standing ** slope) + 1 for standing in range(1, number_of + 1)]
    largest = reach if full else min(reach, max(-(-total // number_of), total * weights[0] // sum(weights)))
    least = 1 if total - largest >= number_of - 1 else 0
    counts, spare = [largest] + [least] * (number_of - 1), total - largest - least * (number_of - 1)
    while spare > 0:
        movable = [i for i in range(1, number_of) if counts[i] < largest] or [i for i in range(1, number_of) if counts[i] < reach]
        mass, budget = sum([weights[i] for i in movable]), spare
        for i in movable:
            more = min(reach - counts[i], max(1, budget * weights[i] // mass), spare)
            counts[i] = counts[i] + more
            spare = spare - more
    return np.array(counts)


def noise(key, dims, deviation, reach, cuts=(), held_as=jnp.bfloat16):
    entries = deviation * jax.random.normal(key, dims, jnp.float32)
    if cuts:
        entries = entries * shard_levels(key, dims, cuts, -0.22, 0.18)
    return jnp.clip(entries, -reach, reach).astype(held_as)


def setup_inputs(seed: int = 0) -> dict:
    splits = jax.random.split(jax.random.key(seed), 7)
    queries = draw_queries(jax.random.fold_in(splits[6], 71), 0)
    keys = draw_keys(jax.random.fold_in(splits[6], 71), 0)
    values = noise(splits[2], (SEQS, LEN, H * DH), 1.0, 6.0, ((0, 4), (1, 8)))
    out_grad = noise(splits[3], (SEQS, LEN, H * DH), 1.0, 6.0, ((0, 4), (1, 8)))
    cluster_ids_keys = jax.random.split(jax.random.fold_in(splits[4], 1), SEQS * H * LEN // TOK_DEV)
    cluster_ids_turns = jax.random.permutation(jax.random.fold_in(splits[4], 3), SEQS * H * LEN // TOK_DEV)
    cluster_ids = jax.vmap(lambda own, number: routed_block(jax.random.fold_in(splits[4], 2), own, number, TOK_DEV, CLUSTERS, 1, CAP, 2))(cluster_ids_keys, cluster_ids_turns).reshape((SEQS, H, LEN, 1))
    centroids = noise(splits[5], (H, CLUSTERS, DH), 1.0, 6.0, (), jnp.float32)
    return dict(queries=queries, keys=keys, values=values, out_grad=out_grad, cluster_ids=cluster_ids, centroids=centroids)


decay_rate = 0.99

def grads_one(blocks_in):
    rows, live_mask = blocks_in
    head_width = rows.shape[-1] // 4
    score_scale = 1.0 / math.sqrt(head_width)
    query_rows = rows[:, :head_width]
    key_rows = rows[:, head_width:2 * head_width]
    value_rows = rows[:, 2 * head_width:3 * head_width]
    grad_rows = rows[:, 3 * head_width:]
    slot_count = rows.shape[0]
    row_ids = lax.broadcasted_iota(jnp.int32, (slot_count, slot_count), 0)
    col_ids = lax.broadcasted_iota(jnp.int32, (slot_count, slot_count), 1)
    allowed = (col_ids <= row_ids) & (live_mask[None, :] | (col_ids == row_ids))
    scores = jnp.dot(query_rows, key_rows.T, preferred_element_type=jnp.float32) * score_scale
    scores = jnp.where(allowed, scores, -1e+30)
    row_max = lax.optimization_barrier(jnp.max(scores, axis=-1, keepdims=True))
    weights_raw = jnp.exp(scores - row_max)
    probs_full = weights_raw / lax.optimization_barrier(jnp.sum(weights_raw, axis=-1, keepdims=True))
    probs_low = probs_full.astype(jnp.bfloat16)
    attended = jnp.dot(probs_low, value_rows, preferred_element_type=jnp.float32)
    row_delta = lax.optimization_barrier(jnp.sum(grad_rows.astype(jnp.float32) * attended, axis=-1, keepdims=True))
    dprobs = jnp.dot(grad_rows, value_rows.T, preferred_element_type=jnp.float32)
    dscores = (probs_full * (dprobs - row_delta)).astype(jnp.bfloat16)
    dquery = jnp.dot(dscores, key_rows, preferred_element_type=jnp.float32) * score_scale
    grad_key = jnp.dot(dscores.T, query_rows, preferred_element_type=jnp.float32) * score_scale
    dvalue = jnp.dot(probs_low.T, grad_rows, preferred_element_type=jnp.float32)
    return jnp.concatenate([dquery, grad_key, dvalue], axis=-1).astype(jnp.bfloat16)

def reference(queries, keys, values, out_grad, cluster_ids, centroids):
    seq_count = queries.shape[0]
    seq_len = queries.shape[1]
    slot_rows = N_CTX * CAP
    stacked = jnp.concatenate([source_arr.reshape(seq_count, seq_len, H, DH) for source_arr in (queries, keys, values, out_grad)], axis=-1)
    packed = jnp.transpose(stacked, (0, 2, 1, 3)).reshape(seq_count * H, seq_len, 4 * DH)
    ids_flat = cluster_ids[..., 0].reshape(seq_count * H, seq_len).astype(jnp.int32)

    def one_pair(pair_in):
        rows, ids_row = pair_in
        onehot = (ids_row[:, None] == jnp.arange(CLUSTERS, dtype=jnp.int32)[None, :]).astype(jnp.int32)
        blocks = onehot.reshape(N_CTX, TOK_DEV, CLUSTERS)
        before = (jnp.cumsum(blocks, axis=1) - blocks).astype(jnp.int32)
        rank_in = lax.optimization_barrier(jnp.sum(before * blocks, axis=-1)).reshape(seq_len).astype(jnp.int32)
        source = (jnp.arange(seq_len, dtype=jnp.int32) // TOK_DEV).astype(jnp.int32)
        slot_of = (ids_row * slot_rows + source * CAP + rank_in).astype(jnp.int32)
        buffers = jnp.zeros((CLUSTERS * slot_rows, 4 * DH), jnp.bfloat16).at[slot_of].set(rows)
        live = jnp.zeros((CLUSTERS * slot_rows,), jnp.bool_).at[slot_of].set(True)
        grads = lax.map(grads_one, (buffers.reshape(CLUSTERS, slot_rows, 4 * DH), live.reshape(CLUSTERS, slot_rows)))
        back_rows = grads.reshape(CLUSTERS * slot_rows, 3 * DH)[slot_of]
        member = onehot.astype(jnp.bfloat16).T
        sums_two = jnp.dot(member, rows[:, :2 * DH], preferred_element_type=jnp.float32)
        return (back_rows, sums_two[:, :DH] + sums_two[:, DH:])
    back, sums = lax.map(one_pair, (packed, ids_flat))
    back = jnp.transpose(back.reshape(seq_count, H, seq_len, 3 * DH), (0, 2, 1, 3))
    grad_queries = back[..., :DH].reshape(seq_count, seq_len, H * DH)
    grad_keys = back[..., DH:2 * DH].reshape(seq_count, seq_len, H * DH)
    grad_values = back[..., 2 * DH:].reshape(seq_count, seq_len, H * DH)
    member_sums = lax.optimization_barrier(jnp.sum(sums.reshape(seq_count, H, CLUSTERS, DH), axis=0))
    new_centroids = decay_rate * centroids + (1.0 - decay_rate) / 2.0 * member_sums
    return (grad_queries, grad_keys, grad_values, new_centroids)
```

```python
import functools
import math

import jax
import jax.numpy as jnp
from jax import lax
from jax.experimental import pallas as pl
from jax.experimental.pallas import tpu as pltpu
from jax.sharding import PartitionSpec as P

decay_rate = 0.99
NEG = -1e30


def dot(a, b, ca=1, cb=0):
    return lax.dot_general(a, b, (((ca,), (cb,)), ((), ())), preferred_element_type=jnp.float32)


def iota(shape, dim):
    return lax.broadcasted_iota(jnp.int32, shape, dim)


def fill_tables(upper, causal):
    upper[...] = jnp.where(iota(upper.shape, 0) < iota(upper.shape, 1), 1.0, 0.0).astype(jnp.bfloat16)
    causal[...] = jnp.where(iota(causal.shape, 0) <= iota(causal.shape, 1), 0.0, NEG)


def expand_block(rows, ids_row, at, upper, slots, bias, slot_col):
    clusters, _, width = slots.shape
    tok = ids_row.shape[1]
    cap = 2 * tok // clusters
    head = width // 4
    hit = iota((clusters, tok), 0) == ids_row
    onehot = jnp.where(hit, 1.0, 0.0).astype(jnp.bfloat16)
    before = dot(onehot, upper[...])
    rank = jnp.sum(jnp.where(hit, before, 0.0), axis=0, keepdims=True)
    slot = ids_row * cap + rank.astype(jnp.int32)
    for i in range(tok // 128):
        piece = jnp.where(iota((128, 128), 0) == iota((128, 128), 1), slot[:, i * 128 : (i + 1) * 128], 0)
        col = jnp.sum(piece.astype(jnp.float32), axis=1, keepdims=True)
        slot_col[pl.ds(i * 128, 128), :] = jnp.broadcast_to(col, (128, 128)).astype(jnp.int32)
    group = min(clusters, 256 // cap)
    where_to = pl.ds(pl.multiple_of(at * cap, cap), cap)
    for i in range(clusters // group):
        take = jnp.where(iota((group * cap, tok), 0) + i * group * cap == slot, 1.0, 0.0)
        live = jnp.sum(take, axis=1, keepdims=True)
        placed = dot(take.astype(jnp.bfloat16), rows).astype(jnp.bfloat16)
        slots[pl.ds(i * group, group), where_to, :] = placed.reshape(group, cap, width)
        hide = jnp.broadcast_to(jnp.where(live > 0.5, 0.0, NEG), (group * cap, 128))
        bias[pl.ds(i * group, group), where_to, :] = hide.reshape(group, cap, 128)
    sums = dot(onehot, rows[:, : 2 * head])
    return sums[:, :head] + sums[:, head:]


def attend(slots, bias, causal, step):
    clusters, count, width = slots.shape
    head = width // 4
    scale = 1.0 / math.sqrt(head)

    def some(i, carry):
        at = [i * step + j for j in range(step)]
        q = [slots[c, :, :head] for c in at]
        k = [slots[c, :, head : 2 * head] for c in at]
        v = [slots[c, :, 2 * head : 3 * head] for c in at]
        g = [slots[c, :, 3 * head :] for c in at]
        hide = [jnp.concatenate([bias[c]] * (count // 128), axis=1) for c in at]
        s = [dot(b, a, 1, 1) for a, b in zip(q, k)]
        dp = [dot(b, a, 1, 1) for a, b in zip(g, v)]
        s = [a * scale + causal[...] + b for a, b in zip(s, hide)]
        e = [jnp.exp(a - jnp.max(a, axis=0, keepdims=True)) for a in s]
        p = [a * (1.0 / jnp.sum(a, axis=0, keepdims=True)) for a in e]
        low = [a.astype(jnp.bfloat16) for a in p]
        delta = [jnp.sum(a.astype(jnp.float32) * b, axis=0, keepdims=True) for a, b in zip(low, dp)]
        ds = [(a * (b - c)).astype(jnp.bfloat16) for a, b, c in zip(p, dp, delta)]
        dv = [dot(a, b).astype(jnp.bfloat16) for a, b in zip(low, g)]
        dk = [(dot(a, b) * scale).astype(jnp.bfloat16) for a, b in zip(ds, q)]
        dq = [(dot(a, b, 0, 0) * scale).astype(jnp.bfloat16) for a, b in zip(ds, k)]
        for j, c in enumerate(at):
            slots[c, :, :head] = dq[j]
            slots[c, :, head : 2 * head] = dk[j]
            slots[c, :, 2 * head : 3 * head] = dv[j]
        return carry

    lax.fori_loop(0, clusters // step, some, 0)


def collect_block(at, slots, slot_col, write):
    clusters, _, width = slots.shape
    tok = slot_col.shape[0]
    cap = 2 * tok // clusters
    keep = 3 * (width // 4)
    grads = slots[:, pl.ds(pl.multiple_of(at * cap, cap), cap), :keep].reshape(clusters * cap, keep)
    rows = min(tok, 256)
    for i in range(tok // rows):
        col = slot_col[pl.ds(i * rows, rows), :]
        col = jnp.concatenate([col] * (clusters * cap // 128), axis=1)
        take = jnp.where(col == iota((rows, clusters * cap), 1), 1.0, 0.0).astype(jnp.bfloat16)
        write(i * rows, dot(take, grads).astype(jnp.bfloat16))


def head_kernel(x, ids, out, sums, slots, bias, slot_col, upper, causal):
    n = x.shape[0]
    fill_tables(upper, causal)
    sums[...] = jnp.zeros_like(sums)

    def into(b, carry):
        sums[...] += expand_block(x[b], ids[b], b, upper, slots, bias, slot_col.at[b])
        return carry

    lax.fori_loop(0, n, into, 0)
    attend(slots, bias, causal, 4)

    def back(b, carry):
        def write(first, rows):
            out[b, pl.ds(first, rows.shape[0]), :] = rows

        collect_block(b, slots, slot_col.at[b], write)
        return carry

    lax.fori_loop(0, n, back, 0)


def head_grads(x, ids, clusters):
    n, tok, width = x.shape
    head = width // 4
    count = n * (2 * tok // clusters)
    vmem = pl.BlockSpec(memory_space=pltpu.VMEM)
    return pl.pallas_call(
        head_kernel,
        out_shape=(
            jax.ShapeDtypeStruct((n, tok, 3 * head), jnp.bfloat16),
            jax.ShapeDtypeStruct((clusters, head), jnp.float32),
        ),
        in_specs=[vmem, vmem],
        out_specs=(vmem, vmem),
        scratch_shapes=[
            pltpu.VMEM((clusters, count, width), jnp.bfloat16),
            pltpu.VMEM((clusters, count, 128), jnp.float32),
            pltpu.VMEM((n, tok, 128), jnp.int32),
            pltpu.VMEM((tok, tok), jnp.bfloat16),
            pltpu.VMEM((count, count), jnp.float32),
        ],
        compiler_params=pltpu.CompilerParams(vmem_limit_bytes=60 * 1024 * 1024),
        cost_estimate=pl.CostEstimate(flops=30_000_000_000, bytes_accessed=8 << 20, transcendentals=0),
    )(x, ids)


def shards(queries, keys, values, out_grad, cluster_ids, centroids):
    tok = queries.shape[1]
    heads = cluster_ids.shape[1]
    head = queries.shape[2] // heads
    clusters = centroids.shape[1]
    n = lax.axis_size("ctx")
    seqs = lax.axis_size("seq")
    own = heads // n
    a2a = functools.partial(lax.all_to_all, axis_name="ctx", split_axis=0, concat_axis=0, tiled=True)
    ids = a2a(cluster_ids.reshape(n, own, tok)).reshape(n, own, 1, tok)
    split = [a[0].reshape(tok, n, own, head) for a in (queries, keys, values, out_grad)]
    arrived = [
        a2a(jnp.transpose(jnp.concatenate([a[:, :, h] for a in split], axis=-1), (1, 0, 2)))
        for h in range(own)
    ]
    done = [head_grads(arrived[h], ids[:, h], clusters) for h in range(own)]
    back = jnp.stack([a2a(d[0]) for d in done], axis=1)
    sums = jnp.stack([d[1] for d in done]).astype(jnp.bfloat16)
    total = sums.astype(jnp.float32)
    for d in range(1, seqs):
        moved = lax.ppermute(sums, "seq", [(i, (i + d) % seqs) for i in range(seqs)])
        total = total + moved.astype(jnp.float32)
    centroid_own = lax.dynamic_slice_in_dim(centroids, lax.axis_index("ctx") * own, own, 0)
    updated = decay_rate * centroid_own + (1.0 - decay_rate) / 2.0 * total
    per_token = jnp.transpose(back, (2, 0, 1, 3))
    grads = [
        per_token[..., i * head : (i + 1) * head].reshape(1, tok, heads * head) for i in range(3)
    ]
    return (*grads, updated)


def solution(mesh):
    split = P("seq", "ctx", None)
    return jax.shard_map(
        shards,
        mesh=mesh,
        in_specs=(split, split, split, split, P("seq", None, "ctx", None), P()),
        out_specs=(split, split, split, P("ctx", None, None)),
        check_vma=False,
    )
```

```python
import functools
import math

import jax
import jax.numpy as jnp
from jax import lax
from jax.experimental import pallas as pl
from jax.experimental.pallas import tpu as pltpu
from jax.sharding import PartitionSpec as P

decay_rate = 0.99
NEG = -1e30


def dot(a, b, ca=1, cb=0):
    return lax.dot_general(a, b, (((ca,), (cb,)), ((), ())), preferred_element_type=jnp.float32)


def iota(shape, dim):
    return lax.broadcasted_iota(jnp.int32, shape, dim)


def fill_tables(upper, causal):
    upper[...] = jnp.where(iota(upper.shape, 0) < iota(upper.shape, 1), 1.0, 0.0).astype(jnp.bfloat16)
    causal[...] = jnp.where(iota(causal.shape, 0) <= iota(causal.shape, 1), 0.0, NEG)


def expand_block(rows, ids_row, at, upper, slots, bias, slot_col):
    clusters, _, width = slots.shape
    tok = ids_row.shape[1]
    cap = 2 * tok // clusters
    head = width // 4
    hit = iota((clusters, tok), 0) == ids_row
    onehot = jnp.where(hit, 1.0, 0.0).astype(jnp.bfloat16)
    before = dot(onehot, upper[...])
    rank = jnp.sum(jnp.where(hit, before, 0.0), axis=0, keepdims=True)
    slot = ids_row * cap + rank.astype(jnp.int32)
    for i in range(tok // 128):
        piece = jnp.where(iota((128, 128), 0) == iota((128, 128), 1), slot[:, i * 128 : (i + 1) * 128], 0)
        col = jnp.sum(piece.astype(jnp.float32), axis=1, keepdims=True)
        slot_col[pl.ds(i * 128, 128), :] = jnp.broadcast_to(col, (128, 128)).astype(jnp.int32)
    group = min(clusters, 256 // cap)
    where_to = pl.ds(pl.multiple_of(at * cap, cap), cap)
    for i in range(clusters // group):
        take = jnp.where(iota((group * cap, tok), 0) + i * group * cap == slot, 1.0, 0.0)
        live = jnp.sum(take, axis=1, keepdims=True)
        placed = dot(take.astype(jnp.bfloat16), rows).astype(jnp.bfloat16)
        slots[pl.ds(i * group, group), where_to, :] = placed.reshape(group, cap, width)
        hide = jnp.broadcast_to(jnp.where(live > 0.5, 0.0, NEG), (group * cap, 128))
        bias[pl.ds(i * group, group), where_to, :] = hide.reshape(group, cap, 128)
    sums = dot(onehot, rows[:, : 2 * head])
    return sums[:, :head] + sums[:, head:]


def attend(slots, bias, causal, step):
    clusters, count, width = slots.shape
    head = width // 4
    scale = 1.0 / math.sqrt(head)

    def some(i, carry):
        at = [i * step + j for j in range(step)]
        q = [slots[c, :, :head] for c in at]
        k = [slots[c, :, head : 2 * head] for c in at]
        v = [slots[c, :, 2 * head : 3 * head] for c in at]
        g = [slots[c, :, 3 * head :] for c in at]
        hide = [jnp.concatenate([bias[c]] * (count // 128), axis=1) for c in at]
        s = [dot(b, a, 1, 1) for a, b in zip(q, k)]
        dp = [dot(b, a, 1, 1) for a, b in zip(g, v)]
        s = [a * scale + causal[...] + b for a, b in zip(s, hide)]
        e = [jnp.exp(a - jnp.max(a, axis=0, keepdims=True)) for a in s]
        p = [a * (1.0 / jnp.sum(a, axis=0, keepdims=True)) for a in e]
        low = [a.astype(jnp.bfloat16) for a in p]
        delta = [jnp.sum(a.astype(jnp.float32) * b, axis=0, keepdims=True) for a, b in zip(low, dp)]
        ds = [(a * (b - c)).astype(jnp.bfloat16) for a, b, c in zip(p, dp, delta)]
        dv = [dot(a, b).astype(jnp.bfloat16) for a, b in zip(low, g)]
        dk = [(dot(a, b) * scale).astype(jnp.bfloat16) for a, b in zip(ds, q)]
        dq = [(dot(a, b, 0, 0) * scale).astype(jnp.bfloat16) for a, b in zip(ds, k)]
        for j, c in enumerate(at):
            slots[c, :, :head] = dq[j]
            slots[c, :, head : 2 * head] = dk[j]
            slots[c, :, 2 * head : 3 * head] = dv[j]
        return carry

    lax.fori_loop(0, clusters // step, some, 0)


def collect_block(at, slots, slot_col, write):
    clusters, _, width = slots.shape
    tok = slot_col.shape[0]
    cap = 2 * tok // clusters
    keep = 3 * (width // 4)
    grads = slots[:, pl.ds(pl.multiple_of(at * cap, cap), cap), :keep].reshape(clusters * cap, keep)
    rows = min(tok, 256)
    for i in range(tok // rows):
        col = slot_col[pl.ds(i * rows, rows), :]
        col = jnp.concatenate([col] * (clusters * cap // 128), axis=1)
        take = jnp.where(col == iota((rows, clusters * cap), 1), 1.0, 0.0).astype(jnp.bfloat16)
        write(i * rows, dot(take, grads).astype(jnp.bfloat16))


def spread_kernel(n, seqs, own, *refs):
    args, refs = refs[:4], refs[4:]
    ids, grads, total, refs = refs[0], refs[1:4], refs[4], refs[5:]
    (recv, recv_ids, ready, all_sums, sums, slots, bias, slot_col, upper, causal), refs = refs[:10], refs[10:]
    local_sem, ids_local, out_send, out_recv, ids_send, ids_recv, back_local, back_send, back_recv, sum_send, sum_recv = refs
    me, row = lax.axis_index("ctx"), lax.axis_index("seq")
    head = total.shape[2]
    mesh_id = pl.DeviceIdType.MESH

    barrier = pltpu.get_barrier_semaphore()
    for d in range(1, n):
        pl.semaphore_signal(barrier, 1, device_id=(row, lax.rem(me + d, n)), device_id_type=mesh_id)
    for d in range(1, seqs):
        pl.semaphore_signal(barrier, 1, device_id=(lax.rem(row + d, seqs), me), device_id_type=mesh_id)

    def columns(device, h):
        return pl.ds(pl.multiple_of((device * own + h) * head, head), head)

    def own_in(h, i):
        return pltpu.make_async_copy(
            args[i].at[:, columns(me, h)], recv.at[h, me, :, pl.ds(i * head, head)], local_sem.at[h, i]
        )

    def far_in(h, d, i):
        to = lax.rem(me + d, n)
        return pltpu.make_async_remote_copy(
            src_ref=args[i].at[:, columns(to, h)],
            dst_ref=recv.at[h, me, :, pl.ds(i * head, head)],
            send_sem=out_send.at[h, d, i],
            recv_sem=out_recv.at[h, d, i],
            device_id=(row, to),
            device_id_type=mesh_id,
        )

    def far_ids(d):
        to = lax.rem(me + d, n)
        return pltpu.make_async_remote_copy(
            src_ref=ids.at[to],
            dst_ref=recv_ids.at[me],
            send_sem=ids_send.at[d],
            recv_sem=ids_recv.at[d],
            device_id=(row, to),
            device_id_type=mesh_id,
        )

    def own_back(h, i):
        return pltpu.make_async_copy(
            ready.at[h, me, :, pl.ds(i * head, head)], grads[i].at[:, columns(me, h)], back_local.at[h, i]
        )

    def far_back(h, d, i):
        to = lax.rem(me + d, n)
        return pltpu.make_async_remote_copy(
            src_ref=ready.at[h, to, :, pl.ds(i * head, head)],
            dst_ref=grads[i].at[:, columns(me, h)],
            send_sem=back_send.at[h, d, i],
            recv_sem=back_recv.at[h, d, i],
            device_id=(row, to),
            device_id_type=mesh_id,
        )

    def far_sum(h, d):
        return pltpu.make_async_remote_copy(
            src_ref=all_sums.at[h, row],
            dst_ref=all_sums.at[h, row],
            send_sem=sum_send.at[h, d],
            recv_sem=sum_recv.at[h, d],
            device_id=(lax.rem(row + d, seqs), me),
            device_id_type=mesh_id,
        )

    def over(low, high, act):
        def step(d, carry):
            act(d)
            return carry

        lax.fori_loop(low, high, step, 0)

    def each(act, count):
        for i in range(count):
            act(i)

    own_ids = pltpu.make_async_copy(ids.at[me], recv_ids.at[me], ids_local)
    own_ids.start()
    for h in range(own):
        each(lambda i: own_in(h, i).start(), 4)
    pl.semaphore_wait(barrier, n + seqs - 2)
    over(1, n, lambda d: far_ids(d).start())
    for h in range(own):
        over(1, n, lambda d: each(lambda i: far_in(h, d, i).start(), 4))
    fill_tables(upper, causal)
    own_ids.wait()

    for h in range(own):

        def expand(b):
            sums[...] += expand_block(recv[h, b], recv_ids[b, h], b, upper, slots, bias, slot_col.at[b])

        def arrive(d):
            if h == 0:
                far_ids(d).wait_recv()
            each(lambda i: far_in(h, d, i).wait_recv(), 4)
            expand(lax.rem(me - d + n, n))

        def collect(b):
            def write(first, rows):
                ready[h, b, pl.ds(first, rows.shape[0]), :] = rows

            collect_block(b, slots, slot_col.at[b], write)

        def leave(d):
            collect(lax.rem(me + d, n))
            each(lambda i: far_back(h, d - 1, i).start(), 3)

        sums[...] = jnp.zeros_like(sums)
        each(lambda i: own_in(h, i).wait(), 4)
        expand(me)
        over(1, n, arrive)
        all_sums[h, row] = sums[...].astype(jnp.bfloat16)
        attend(slots, bias, causal, 4)
        over(1, seqs, lambda d: far_sum(h, d).start())
        collect(lax.rem(me + 1, n))
        over(2, n, leave)
        collect(me)
        each(lambda i: far_back(h, n - 1, i).start(), 3)
        each(lambda i: own_back(h, i).start(), 3)

    for h in range(own):
        over(1, seqs, lambda d: far_sum(h, d).wait())
        whole = all_sums[h, 0].astype(jnp.float32)
        for s in range(1, seqs):
            whole = whole + all_sums[h, s].astype(jnp.float32)
        total[h] = whole
    over(1, n, lambda d: far_ids(d).wait_send())
    for h in range(own):
        over(1, n, lambda d: each(lambda i: far_in(h, d, i).wait_send(), 4))
        each(lambda i: own_back(h, i).wait(), 3)
        over(1, n, lambda d: each(lambda i: far_back(h, d, i).wait(), 3))


def shards(queries, keys, values, out_grad, cluster_ids, centroids):
    tok = queries.shape[1]
    heads = cluster_ids.shape[1]
    head = queries.shape[2] // heads
    clusters = centroids.shape[1]
    n = lax.axis_size("ctx")
    seqs = lax.axis_size("seq")
    own = heads // n
    count = n * (2 * tok // clusters)
    dma = pltpu.SemaphoreType.DMA
    anywhere = pl.BlockSpec(memory_space=pl.ANY)
    *grads, total = pl.pallas_call(
        functools.partial(spread_kernel, n, seqs, own),
        out_shape=[jax.ShapeDtypeStruct((tok, heads * head), jnp.bfloat16)] * 3
        + [jax.ShapeDtypeStruct((own, clusters, head), jnp.float32)],
        in_specs=[anywhere] * 5,
        out_specs=[anywhere] * 3 + [pl.BlockSpec(memory_space=pltpu.VMEM)],
        scratch_shapes=[
            pltpu.VMEM((own, n, tok, 4 * head), jnp.bfloat16),
            pltpu.VMEM((n, own, 1, tok), jnp.int32),
            pltpu.VMEM((own, n, tok, 3 * head), jnp.bfloat16),
            pltpu.VMEM((own, seqs, clusters, head), jnp.bfloat16),
            pltpu.VMEM((clusters, head), jnp.float32),
            pltpu.VMEM((clusters, count, 4 * head), jnp.bfloat16),
            pltpu.VMEM((clusters, count, 128), jnp.float32),
            pltpu.VMEM((n, tok, 128), jnp.int32),
            pltpu.VMEM((tok, tok), jnp.bfloat16),
            pltpu.VMEM((count, count), jnp.float32),
            dma((own, 4)),
            dma,
            dma((own, n, 4)),
            dma((own, n, 4)),
            dma((n,)),
            dma((n,)),
            dma((own, 3)),
            dma((own, n, 3)),
            dma((own, n, 3)),
            dma((own, seqs)),
            dma((own, seqs)),
        ],
        compiler_params=pltpu.CompilerParams(
            collective_id=0, has_side_effects=True, vmem_limit_bytes=60 * 1024 * 1024
        ),
    )(queries[0], keys[0], values[0], out_grad[0], cluster_ids.reshape(n, own, 1, tok))
    centroid_own = lax.dynamic_slice_in_dim(centroids, lax.axis_index("ctx") * own, own, 0)
    updated = decay_rate * centroid_own + (1.0 - decay_rate) / 2.0 * total
    return (*[a[None] for a in grads], updated)


def solution(mesh):
    split = P("seq", "ctx", None)
    return jax.shard_map(
        shards,
        mesh=mesh,
        in_specs=(split, split, split, split, P("seq", None, "ctx", None), P()),
        out_specs=(split, split, split, P("ctx", None, None)),
        check_vma=False,
    )
```

```python
import functools
import math

import jax
import jax.numpy as jnp
from jax import lax
from jax.experimental import pallas as pl
from jax.experimental.pallas import tpu as pltpu
from jax.sharding import PartitionSpec as P

decay_rate = 0.99
NEG = -1e30


def dot(a, b, ca=1, cb=0):
    return lax.dot_general(a, b, (((ca,), (cb,)), ((), ())), preferred_element_type=jnp.float32)


def iota(shape, dim):
    return lax.broadcasted_iota(jnp.int32, shape, dim)


def fill_tables(upper, causal):
    upper[...] = jnp.where(iota(upper.shape, 0) < iota(upper.shape, 1), 1.0, 0.0).astype(jnp.bfloat16)
    causal[...] = jnp.where(iota(causal.shape, 0) <= iota(causal.shape, 1), 0.0, NEG)


def expand_block(rows, ids_row, at, upper, slots, bias, slot_col):
    clusters, _, width = slots.shape
    tok = ids_row.shape[1]
    cap = 2 * tok // clusters
    head = width // 4
    hit = iota((clusters, tok), 0) == ids_row
    onehot = jnp.where(hit, 1.0, 0.0).astype(jnp.bfloat16)
    before = dot(onehot, upper[...])
    rank = jnp.sum(jnp.where(hit, before, 0.0), axis=0, keepdims=True)
    slot = ids_row * cap + rank.astype(jnp.int32)
    for i in range(tok // 128):
        piece = jnp.where(iota((128, 128), 0) == iota((128, 128), 1), slot[:, i * 128 : (i + 1) * 128], 0)
        col = jnp.sum(piece.astype(jnp.float32), axis=1, keepdims=True)
        slot_col[pl.ds(i * 128, 128), :] = jnp.broadcast_to(col, (128, 128)).astype(jnp.int32)
    group = min(clusters, 256 // cap)
    where_to = pl.ds(pl.multiple_of(at * cap, cap), cap)
    for i in range(clusters // group):
        take = jnp.where(iota((group * cap, tok), 0) + i * group * cap == slot, 1.0, 0.0)
        live = jnp.sum(take, axis=1, keepdims=True)
        placed = dot(take.astype(jnp.bfloat16), rows).astype(jnp.bfloat16)
        slots[pl.ds(i * group, group), where_to, :] = placed.reshape(group, cap, width)
        hide = jnp.broadcast_to(jnp.where(live > 0.5, 0.0, NEG), (group * cap, 128))
        bias[pl.ds(i * group, group), where_to, :] = hide.reshape(group, cap, 128)
    sums = dot(onehot, rows[:, : 2 * head])
    return sums[:, :head] + sums[:, head:]


def attend(slots, bias, causal, step):
    clusters, count, width = slots.shape
    head = width // 4
    scale = 1.0 / math.sqrt(head)

    def some(i, carry):
        at = [i * step + j for j in range(step)]
        q = [slots[c, :, :head] for c in at]
        k = [slots[c, :, head : 2 * head] for c in at]
        v = [slots[c, :, 2 * head : 3 * head] for c in at]
        g = [slots[c, :, 3 * head :] for c in at]
        hide = [jnp.concatenate([bias[c]] * (count // 128), axis=1) for c in at]
        s = [dot(b, a, 1, 1) for a, b in zip(q, k)]
        dp = [dot(b, a, 1, 1) for a, b in zip(g, v)]
        s = [a * scale + causal[...] + b for a, b in zip(s, hide)]
        e = [jnp.exp(a - jnp.max(a, axis=0, keepdims=True)) for a in s]
        p = [a * (1.0 / jnp.sum(a, axis=0, keepdims=True)) for a in e]
        low = [a.astype(jnp.bfloat16) for a in p]
        delta = [jnp.sum(a.astype(jnp.float32) * b, axis=0, keepdims=True) for a, b in zip(low, dp)]
        ds = [(a * (b - c)).astype(jnp.bfloat16) for a, b, c in zip(p, dp, delta)]
        dv = [dot(a, b).astype(jnp.bfloat16) for a, b in zip(low, g)]
        dk = [(dot(a, b) * scale).astype(jnp.bfloat16) for a, b in zip(ds, q)]
        dq = [(dot(a, b, 0, 0) * scale).astype(jnp.bfloat16) for a, b in zip(ds, k)]
        for j, c in enumerate(at):
            slots[c, :, :head] = dq[j]
            slots[c, :, head : 2 * head] = dk[j]
            slots[c, :, 2 * head : 3 * head] = dv[j]
        return carry

    lax.fori_loop(0, clusters // step, some, 0)


def collect_block(at, slots, slot_col, write):
    clusters, _, width = slots.shape
    tok = slot_col.shape[0]
    cap = 2 * tok // clusters
    keep = 3 * (width // 4)
    grads = slots[:, pl.ds(pl.multiple_of(at * cap, cap), cap), :keep].reshape(clusters * cap, keep)
    rows = min(tok, 256)
    for i in range(tok // rows):
        col = slot_col[pl.ds(i * rows, rows), :]
        col = jnp.concatenate([col] * (clusters * cap // 128), axis=1)
        take = jnp.where(col == iota((rows, clusters * cap), 1), 1.0, 0.0).astype(jnp.bfloat16)
        write(i * rows, dot(take, grads).astype(jnp.bfloat16))


def spread_kernel(n, seqs, own, *refs):
    args, refs = refs[:4], refs[4:]
    ids, grads, total, refs = refs[0], refs[1:4], refs[4], refs[5:]
    (recv, recv_ids, ready, all_sums, sums, slots, bias, slot_col, upper, causal), refs = refs[:10], refs[10:]
    local_sem, ids_local, out_send, out_recv, ids_send, ids_recv, back_local, back_send, back_recv, sum_send, sum_recv = refs
    me, row = lax.axis_index("ctx"), lax.axis_index("seq")
    head = total.shape[2]
    mesh_id = pl.DeviceIdType.MESH

    barrier = pltpu.get_barrier_semaphore()
    for d in range(1, n):
        pl.semaphore_signal(barrier, 1, device_id=(row, lax.rem(me + d, n)), device_id_type=mesh_id)
    for d in range(1, seqs):
        pl.semaphore_signal(barrier, 1, device_id=(lax.rem(row + d, seqs), me), device_id_type=mesh_id)

    def columns(device, h):
        return pl.ds(pl.multiple_of((device * own + h) * head, head), head)

    def own_in(h, i):
        return pltpu.make_async_copy(
            args[i].at[:, columns(me, h)], recv.at[h, me, i], local_sem.at[h, i]
        )

    def far_in(h, d, i):
        to = lax.rem(me + d, n)
        return pltpu.make_async_remote_copy(
            src_ref=args[i].at[:, columns(to, h)],
            dst_ref=recv.at[h, me, i],
            send_sem=out_send.at[h, d, i],
            recv_sem=out_recv.at[h, d, i],
            device_id=(row, to),
            device_id_type=mesh_id,
        )

    def far_ids(d):
        to = lax.rem(me + d, n)
        return pltpu.make_async_remote_copy(
            src_ref=ids.at[to],
            dst_ref=recv_ids.at[me],
            send_sem=ids_send.at[d],
            recv_sem=ids_recv.at[d],
            device_id=(row, to),
            device_id_type=mesh_id,
        )

    def own_back(h, i):
        return pltpu.make_async_copy(
            ready.at[h, me, i], grads[i].at[:, columns(me, h)], back_local.at[h, i]
        )

    def far_back(h, d, i):
        to = lax.rem(me + d, n)
        return pltpu.make_async_remote_copy(
            src_ref=ready.at[h, to, i],
            dst_ref=grads[i].at[:, columns(me, h)],
            send_sem=back_send.at[h, d, i],
            recv_sem=back_recv.at[h, d, i],
            device_id=(row, to),
            device_id_type=mesh_id,
        )

    def far_sum(h, d):
        return pltpu.make_async_remote_copy(
            src_ref=all_sums.at[h, row],
            dst_ref=all_sums.at[h, row],
            send_sem=sum_send.at[h, d],
            recv_sem=sum_recv.at[h, d],
            device_id=(lax.rem(row + d, seqs), me),
            device_id_type=mesh_id,
        )

    def over(low, high, act):
        def step(d, carry):
            act(d)
            return carry

        lax.fori_loop(low, high, step, 0)

    def each(act, count):
        for i in range(count):
            act(i)

    own_ids = pltpu.make_async_copy(ids.at[me], recv_ids.at[me], ids_local)
    own_ids.start()
    for h in range(own):
        each(lambda i: own_in(h, i).start(), 4)
    pl.semaphore_wait(barrier, n + seqs - 2)
    over(1, n, lambda d: far_ids(d).start())
    for h in range(own):
        over(1, n, lambda d: each(lambda i: far_in(h, d, i).start(), 4))
    fill_tables(upper, causal)
    own_ids.wait()

    for h in range(own):

        def expand(b):
            sums[...] += expand_block(jnp.concatenate([recv[h, b, i] for i in range(4)], axis=1), recv_ids[b, h], b, upper, slots, bias, slot_col.at[b])

        def arrive(d):
            if h == 0:
                far_ids(d).wait_recv()
            each(lambda i: far_in(h, d, i).wait_recv(), 4)
            expand(lax.rem(me - d + n, n))

        def collect(b):
            def write(first, rows):
                for i in range(3):
                    ready[h, b, i, pl.ds(first, rows.shape[0]), :] = rows[:, i * head : (i + 1) * head]

            collect_block(b, slots, slot_col.at[b], write)

        def leave(d):
            collect(lax.rem(me + d, n))
            each(lambda i: far_back(h, d - 1, i).start(), 3)

        sums[...] = jnp.zeros_like(sums)
        each(lambda i: own_in(h, i).wait(), 4)
        expand(me)
        over(1, n, arrive)
        all_sums[h, row] = sums[...].astype(jnp.bfloat16)
        attend(slots, bias, causal, 4)
        over(1, seqs, lambda d: far_sum(h, d).start())
        collect(lax.rem(me + 1, n))
        over(2, n, leave)
        collect(me)
        each(lambda i: far_back(h, n - 1, i).start(), 3)
        each(lambda i: own_back(h, i).start(), 3)

    for h in range(own):
        over(1, seqs, lambda d: far_sum(h, d).wait())
        whole = all_sums[h, 0].astype(jnp.float32)
        for s in range(1, seqs):
            whole = whole + all_sums[h, s].astype(jnp.float32)
        total[h] = whole
    over(1, n, lambda d: far_ids(d).wait_send())
    for h in range(own):
        over(1, n, lambda d: each(lambda i: far_in(h, d, i).wait_send(), 4))
        each(lambda i: own_back(h, i).wait(), 3)
        over(1, n, lambda d: each(lambda i: far_back(h, d, i).wait(), 3))


def shards(queries, keys, values, out_grad, cluster_ids, centroids):
    tok = queries.shape[1]
    heads = cluster_ids.shape[1]
    head = queries.shape[2] // heads
    clusters = centroids.shape[1]
    n = lax.axis_size("ctx")
    seqs = lax.axis_size("seq")
    own = heads // n
    count = n * (2 * tok // clusters)
    dma = pltpu.SemaphoreType.DMA
    anywhere = pl.BlockSpec(memory_space=pl.ANY)
    *grads, total = pl.pallas_call(
        functools.partial(spread_kernel, n, seqs, own),
        out_shape=[jax.ShapeDtypeStruct((tok, heads * head), jnp.bfloat16)] * 3
        + [jax.ShapeDtypeStruct((own, clusters, head), jnp.float32)],
        in_specs=[anywhere] * 5,
        out_specs=[anywhere] * 3 + [pl.BlockSpec(memory_space=pltpu.VMEM)],
        scratch_shapes=[
            pltpu.VMEM((own, n, 4, tok, head), jnp.bfloat16),
            pltpu.VMEM((n, own, 1, tok), jnp.int32),
            pltpu.VMEM((own, n, 3, tok, head), jnp.bfloat16),
            pltpu.VMEM((own, seqs, clusters, head), jnp.bfloat16),
            pltpu.VMEM((clusters, head), jnp.float32),
            pltpu.VMEM((clusters, count, 4 * head), jnp.bfloat16),
            pltpu.VMEM((clusters, count, 128), jnp.float32),
            pltpu.VMEM((n, tok, 128), jnp.int32),
            pltpu.VMEM((tok, tok), jnp.bfloat16),
            pltpu.VMEM((count, count), jnp.float32),
            dma((own, 4)),
            dma,
            dma((own, n, 4)),
            dma((own, n, 4)),
            dma((n,)),
            dma((n,)),
            dma((own, 3)),
            dma((own, n, 3)),
            dma((own, n, 3)),
            dma((own, seqs)),
            dma((own, seqs)),
        ],
        compiler_params=pltpu.CompilerParams(
            collective_id=0, has_side_effects=True, vmem_limit_bytes=60 * 1024 * 1024
        ),
    )(queries[0], keys[0], values[0], out_grad[0], cluster_ids.reshape(n, own, 1, tok))
    centroid_own = lax.dynamic_slice_in_dim(centroids, lax.axis_index("ctx") * own, own, 0)
    updated = decay_rate * centroid_own + (1.0 - decay_rate) / 2.0 * total
    return (*[a[None] for a in grads], updated)


def solution(mesh):
    split = P("seq", "ctx", None)
    return jax.shard_map(
        shards,
        mesh=mesh,
        in_specs=(split, split, split, split, P("seq", None, "ctx", None), P()),
        out_specs=(split, split, split, P("ctx", None, None)),
        check_vma=False,
    )
```
